32 devices in a mesh: ax: 4 (over x, core), ay: 8 (over z, y).
Axes of the slice: x: 2, y: 2, z: 4, core: 2. Of those that a mesh axis runs over, the one named last changes fastest.
Arguments:
- matrices: bfloat16 [256, 512, 512], P(('ax', 'ay')), as said below
- basis_cols: bfloat16 [256, 512, 384], P(('ax', 'ay')), may hold values from -6 to 6
- mode_counts: int32 [256], P(('ax', 'ay')), may hold values from 64 to 384
- task_map: int32 [256], P(('ax', 'ay')), may hold values from 0 to 7, as said below
- neighbour: int32 [256], P(('ax', 'ay')), may hold values from 0 to 7
Outputs:
- smoothed: bfloat16 [256, 512, 384], P(('ax', 'ay'))
- coarse: bfloat16 [256, 384, 384], P(('ax', 'ay'))
The draws below stay inside these ranges and needn't reach their ends.
Inputs may be any that keep to these rules, and one draw needn't show every extreme that they name: `task_map`: each block of 8 consecutive entries (the agglomerates of one device) holds every ay index exactly once. `matrices`: symmetric with a positive diagonal.
All inputs are finite; a program needn't handle non-finite values.
Results may differ from the reference program's by a relative error of at most 0.0066.
Values may be sent and summed in bfloat16 or wider, within the bound.
No kernel may reach another device: no remote copies, remote signals or barrier semaphores. Data moves between devices by JAX's collectives and lax.ppermute only.
A program may use at most 128 MiB of HBM per device.

```python
import math
import jax
import jax.numpy as jnp
from jax import lax

U = 512
M = 384
TILE = 128
AGG_DEV = 8
AGG = 256
N_AY = 8


def draw_matrices(key, part):
    first, second = jax.random.split(key)
    noise = jax.random.normal(first, (AGG, U, U), jnp.float32)
    diag_part = 2.0 + 1.5 * jax.random.uniform(second, (AGG, U), jnp.float32)
    sigma = 0.7 / math.sqrt(U)
    sym = (noise + jnp.swapaxes(noise, 1, 2)) * (sigma / math.sqrt(2.0))
    eye = jnp.eye(U, dtype=jnp.float32)
    return (sym + eye[None, :, :] * diag_part[:, :, None]).astype(jnp.bfloat16)


def draw_mode_counts(key, part):
    first, second, third = jax.random.split(jax.random.fold_in(key, 11), 3)
    groups = M // TILE
    devices = AGG // AGG_DEV
    level = jax.random.randint(first, (devices, 1), 1, groups + 1)
    tiles = jnp.clip(level + jax.random.randint(second, (devices, AGG_DEV), -1, 2), 1, groups)
    within = jax.random.randint(third, (devices, AGG_DEV), TILE // 2, TILE + 1)
    counts = ((tiles - 1) * TILE + within).reshape(-1)
    index = jnp.arange(AGG, dtype=jnp.int32)
    counts = jnp.where(index == 0, M, counts)
    counts = jnp.where(index == 1, TILE // 2, counts)
    return counts.astype(jnp.int32)


def draw_task_map(key, part):
    keys = jax.random.split(jax.random.fold_in(key, 23), AGG // AGG_DEV)
    perms = jax.vmap(lambda single: jax.random.permutation(single, AGG_DEV))(keys)
    return perms.reshape(-1).astype(jnp.int32)


def set_ends(values, rng, smallest, high):
    dims = values.shape
    index_at = [jax.random.randint(jax.random.fold_in(rng, axis), (), 0, dims[axis]) for axis in range(len(dims))]
    values = values.at[tuple(index_at)].set(smallest)
    longest = dims.index(max(dims))
    index_at[longest] = (index_at[longest] + 1) % dims[longest]
    return values.at[tuple(index_at)].set(high)


def steps_of(rng, shape, cuts, least, top_value):
    loudness, own = 1.0, jax.random.fold_in(rng, 6)
    for axis_at, blocks in cuts:
        heights = jnp.exp(jax.random.uniform(jax.random.fold_in(own, axis_at), (blocks,), jnp.float32, least / len(cuts), top_value / len(cuts)))
        loudness = loudness * jnp.repeat(heights, shape[axis_at] // blocks).reshape([-1 if axis == axis_at else 1 for axis in range(len(shape))])
    return loudness


def bell_draw(rng, dims, deviation, reach, shards=(), kind=jnp.bfloat16):
    factor_of = steps_of(rng, dims, shards, -0.22, 0.18) if shards else 1.0
    values = jax.random.normal(rng, dims, jnp.float32) * deviation * factor_of
    return jnp.minimum(jnp.maximum(values, -reach), reach).astype(kind)


def setup_inputs(seed: int = 0) -> dict:
    arg_keys = jax.random.split(jax.random.key(seed), 6)
    return {
        "matrices": draw_matrices(jax.random.fold_in(arg_keys[5], 71), 0),
        "basis_cols": bell_draw(arg_keys[1], (AGG, U, M), 1.0, 6.0, ((0, 32),)),
        "mode_counts": draw_mode_counts(jax.random.fold_in(arg_keys[5], 71), 0),
        "task_map": draw_task_map(jax.random.fold_in(arg_keys[5], 71), 0),
        "neighbour": set_ends(jax.random.randint(arg_keys[4], (AGG,), 0, AGG_DEV), jax.random.fold_in(arg_keys[4], 1), 0, AGG_DEV - 1).astype(jnp.int32),
    }


omegas = (0.3, 0.25, 0.2, 0.3, 0.25, 0.2)

def smooth_one(matrix, columns_in, live):

    def tile_step(tile, carry):
        result, applied = carry
        start = (tile * TILE).astype(jnp.int32)
        current = lax.dynamic_slice_in_dim(columns_in, start, TILE, 1)
        for weight in omegas:
            product = jnp.dot(matrix, current, preferred_element_type=jnp.float32)
            current = (current.astype(jnp.float32) - weight * product).astype(columns_in.dtype)
        image = jnp.dot(matrix, current, preferred_element_type=jnp.float32).astype(columns_in.dtype)
        result = lax.dynamic_update_slice_in_dim(result, current, start, 1)
        applied = lax.dynamic_update_slice_in_dim(applied, image, start, 1)
        return (result, applied)
    zeros = jnp.zeros(columns_in.shape, columns_in.dtype)
    return lax.fori_loop(jnp.int32(0), live, tile_step, (zeros, zeros))

def reference(matrices, basis_cols, mode_counts, task_map, neighbour):
    total = matrices.shape[0]
    width = matrices.shape[1]
    scale = 1.0 / math.sqrt(width)

    def smooth_item(item):
        matrix, columns, count = item
        keep = jnp.arange(columns.shape[1], dtype=jnp.int32) < count
        columns = jnp.where(keep[None, :], columns, jnp.zeros_like(columns))
        live = ((count + TILE - 1) // TILE).astype(jnp.int32)
        return smooth_one(matrix, columns, live)
    smoothed, image = lax.map(smooth_item, (matrices, basis_cols, mode_counts))
    index = jnp.arange(total, dtype=jnp.int32)
    device = index // AGG_DEV
    row_index = device // N_AY
    col_index = device % N_AY
    lower = ((row_index - 1) * N_AY + col_index) * AGG_DEV + neighbour
    valid = row_index >= 1
    lower = jnp.where(valid, lower, 0).astype(jnp.int32)

    def block_item(item):
        applied, low, present, result = item
        partner = smoothed[low]
        partner = jnp.where(present, partner, jnp.zeros_like(partner))
        own = jnp.einsum('um,un->mn', result.astype(jnp.float32), applied.astype(jnp.float32))
        pair = jnp.einsum('um,un->mn', applied.astype(jnp.float32), partner.astype(jnp.float32)).astype(result.dtype)
        return ((own + pair.astype(jnp.float32)) * scale).astype(result.dtype)
    blocks = lax.map(block_item, (image, lower, valid, smoothed))
    target = ((row_index * N_AY + task_map) * AGG_DEV + col_index).astype(jnp.int32)
    coarse = jnp.zeros_like(blocks).at[target].set(blocks)
    return (smoothed, coarse)
```

```python
import functools
import math

import jax
import jax.numpy as jnp
from jax import lax
from jax.experimental import pallas as pl
from jax.experimental.pallas import tpu as pltpu
from jax.sharding import PartitionSpec as P


TILE = 128
CHUNKS = 4
omegas = (0.3, 0.25, 0.2, 0.3, 0.25, 0.2)

ANY = pl.BlockSpec(memory_space=pltpu.HBM)


def smooth_kernel(slots, counts, a_ref, b_ref, *refs):
    full_ref, x_ref, y_ref = refs[-3:]
    width, modes = b_ref.shape[1:]
    count = counts[slots[pl.program_id(0)]]
    groups = pl.cdiv(count, TILE)
    for live in range(1, modes // TILE + 1):

        @pl.when(groups == live)
        def _():
            top = live * TILE
            a = a_ref[0]
            rows = lax.broadcasted_iota(jnp.int32, (top, width), 0)
            start = jnp.where(rows < count, b_ref[0, :, :top].T, jnp.zeros((), jnp.bfloat16))
            current = [start[i * TILE : (i + 1) * TILE] for i in range(live)]
            for weight in omegas:
                product = [jnp.dot(c, a, preferred_element_type=jnp.float32) for c in current]
                current = [
                    (c.astype(jnp.float32) - weight * p).astype(jnp.bfloat16)
                    for c, p in zip(current, product)
                ]
            for i, c in enumerate(current):
                image = jnp.dot(c, a, preferred_element_type=jnp.float32)
                y_ref[0, i * TILE : (i + 1) * TILE, :] = image.astype(jnp.bfloat16)
                x_ref[0, :, i * TILE : (i + 1) * TILE] = c.T
            if top < modes:
                y_ref[0, top:, :] = jnp.zeros((modes - top, width), jnp.bfloat16)
                x_ref[0, :, top:] = jnp.zeros((width, modes - top), jnp.bfloat16)
    full_ref[...] = x_ref[...]


def smooth(slots, counts, matrices, basis, full):
    n = slots.shape[0]
    total, width, modes = basis.shape
    picked = lambda i, s, c: (s[i], 0, 0)
    plain = lambda i, s, c: (i, 0, 0)
    chained = [] if full is None else [full]
    return pl.pallas_call(
        smooth_kernel,
        grid_spec=pltpu.PrefetchScalarGridSpec(
            num_scalar_prefetch=2,
            grid=(n,),
            in_specs=[
                pl.BlockSpec((1, width, width), picked),
                pl.BlockSpec((1, width, modes), picked),
            ]
            + [ANY] * len(chained),
            out_specs=[
                pl.BlockSpec((1, width, modes), picked),
                pl.BlockSpec((1, width, modes), plain),
                pl.BlockSpec((1, modes, width), plain),
            ],
        ),
        out_shape=[
            jax.ShapeDtypeStruct((total, width, modes), jnp.bfloat16),
            jax.ShapeDtypeStruct((n, width, modes), jnp.bfloat16),
            jax.ShapeDtypeStruct((n, modes, width), jnp.bfloat16),
        ],
        input_output_aliases={} if full is None else {4: 0},
        cost_estimate=pl.CostEstimate(
            flops=14 * n * width * width * modes,
            bytes_accessed=2 * n * width * (width + 4 * modes),
            transcendentals=0,
        ),
    )(slots, counts, matrices, basis, *chained)


def block_kernel(steps, parts, partner, me, task, neighbour, *refs):
    scale = 1.0 / math.sqrt(refs[0].shape[1])
    xs, ys, lows = refs[:parts], refs[parts : 2 * parts], refs[2 * parts : 3 * parts]
    outs = refs[3 * parts : 3 * parts + len(steps)]
    x_buf, y_buf, low_buf, sems = refs[3 * parts + len(steps) :]
    each = xs[0].shape[0]

    def load(i):
        target = partner(me[0], steps[i])
        g = jnp.int32(0)
        for s in range(parts * each):
            g = jnp.where(task[s] == target, s, g)
        h = neighbour[g]
        at = i % 2
        for part in range(parts):

            @pl.when(g // each == part)
            def _():
                pltpu.make_async_copy(xs[part].at[g % each], x_buf.at[at], sems.at[0, at]).start()
                pltpu.make_async_copy(ys[part].at[g % each], y_buf.at[at], sems.at[1, at]).start()

            @pl.when(h // each == part)
            def _():
                pltpu.make_async_copy(
                    lows[part].at[h % each], low_buf.at[at], sems.at[2, at]
                ).start()

    load(0)
    for i, out in enumerate(outs):
        at = i % 2
        if i + 1 < len(outs):
            load(i + 1)
        pltpu.make_async_copy(xs[0].at[0], x_buf.at[at], sems.at[0, at]).wait()
        pltpu.make_async_copy(ys[0].at[0], y_buf.at[at], sems.at[1, at]).wait()
        pltpu.make_async_copy(lows[0].at[0], low_buf.at[at], sems.at[2, at]).wait()
        y = y_buf[at]
        pair = jnp.dot(y, low_buf[at], preferred_element_type=jnp.float32).astype(jnp.bfloat16)
        own = jnp.dot(y, x_buf[at], preferred_element_type=jnp.float32)
        out[0] = ((own + pair.astype(jnp.float32)) * scale).astype(jnp.bfloat16)


def blocks(steps, partner, me, task, neighbour, xs, ys, lows):
    width, modes = xs[0].shape[1:]
    parts = len(xs)
    smem = pl.BlockSpec(memory_space=pltpu.SMEM)
    shape = (1, modes, modes)
    return pl.pallas_call(
        functools.partial(block_kernel, steps, parts, partner),
        in_specs=[smem] * 3 + [ANY] * (3 * parts),
        out_specs=[pl.BlockSpec(memory_space=pltpu.VMEM)] * len(steps),
        out_shape=[jax.ShapeDtypeStruct(shape, jnp.bfloat16)] * len(steps),
        scratch_shapes=[
            pltpu.VMEM((2, width, modes), jnp.bfloat16),
            pltpu.VMEM((2, modes, width), jnp.bfloat16),
            pltpu.VMEM((2, width, modes), jnp.bfloat16),
            pltpu.SemaphoreType.DMA((3, 2)),
        ],
        cost_estimate=pl.CostEstimate(
            flops=4 * len(steps) * width * modes * modes,
            bytes_accessed=2 * len(steps) * modes * (3 * width + modes),
            transcendentals=0,
        ),
    )(me, task, neighbour, *xs, *ys, *lows)


def body(matrices, basis_cols, mode_counts, task_map, neighbour):
    count, width, modes = basis_cols.shape
    columns, rows = lax.axis_size("ay"), lax.axis_size("ax")
    me = lax.axis_index("ay")
    paired = columns & (columns - 1) == 0
    partner = (lambda c, k: c ^ k) if paired else (lambda c, k: lax.rem(c + k, columns))
    source = (lambda c, k: c ^ k) if paired else (lambda c, k: lax.rem(c - k + columns, columns))
    each = count // CHUNKS
    up = [(i, i + 1) for i in range(rows - 1)]

    full, xs, ys, lows = None, [], [], []
    for part in range(CHUNKS):
        slots = jnp.arange(part * each, (part + 1) * each, dtype=jnp.int32)
        full, x, y = smooth(slots, mode_counts, matrices, basis_cols, full)
        xs.append(x)
        ys.append(y)
        lows.append(lax.ppermute(x, "ax", up))

    half = columns // 2
    first, second = tuple(range(half, columns)), tuple(range(half - 1, -1, -1))
    mine = me.astype(jnp.int32).reshape(1)
    coarse = jnp.zeros((count, modes, modes), jnp.bfloat16)
    arrived = []
    for steps in (first, second):
        made = blocks(steps, partner, mine, task_map, neighbour, xs, ys, lows)
        for k, block in zip(steps, made):
            if k:
                pairs = [(i, int(i ^ k) if paired else (i + k) % columns) for i in range(columns)]
                block = lax.ppermute(block, "ay", pairs)
            arrived.append((k, block))
    for k, block in arrived[-1:] + arrived[:-1]:
        coarse = lax.dynamic_update_slice(coarse, block, (source(me, k), 0, 0))
    return full, coarse


def solution(mesh):
    agg = P(("ax", "ay"), None, None)
    flat = P(("ax", "ay"))
    return jax.shard_map(
        body,
        mesh=mesh,
        in_specs=(agg, agg, flat, flat, flat),
        out_specs=(agg, agg),
        check_vma=False,
    )
```

```python
import functools
import math

import jax
import jax.numpy as jnp
from jax import lax
from jax.experimental import pallas as pl
from jax.experimental.pallas import tpu as pltpu
from jax.sharding import PartitionSpec as P


TILE = 128
omegas = (0.3, 0.25, 0.2, 0.3, 0.25, 0.2)

SMEM = pl.BlockSpec(memory_space=pltpu.SMEM)
VMEM = pl.BlockSpec(memory_space=pltpu.VMEM)
HBM = pl.BlockSpec(memory_space=pltpu.HBM)
ANY = pl.BlockSpec(memory_space=pl.ANY)


def in_vmem(array):
    return pltpu.with_memory_space_constraint(array, pltpu.VMEM)


def smooth_kernel(counts, a_ref, b_ref, x_ref, y_ref):
    slots, width, modes = b_ref.shape
    mine = [counts[pl.program_id(0) * slots + s] for s in range(slots)]
    groups = pl.cdiv(functools.reduce(jnp.maximum, mine), TILE)
    for live in range(1, modes // TILE + 1):

        @pl.when(groups == live)
        def _():
            top = live * TILE
            rows = lax.broadcasted_iota(jnp.int32, (top, width), 0)
            zero = jnp.zeros((), jnp.bfloat16)
            current = [
                jnp.where(rows < mine[s], b_ref[s, :, :top].T, zero) for s in range(slots)
            ]
            for weight in omegas:
                product = [
                    jnp.dot(current[s], a_ref[s], preferred_element_type=jnp.float32)
                    for s in range(slots)
                ]
                current = [
                    (c.astype(jnp.float32) - weight * p).astype(jnp.bfloat16)
                    for c, p in zip(current, product)
                ]
            for s, c in enumerate(current):
                image = jnp.dot(c, a_ref[s], preferred_element_type=jnp.float32)
                y_ref[s, :top, :] = image.astype(jnp.bfloat16)
                x_ref[s, :, :top] = c.T
                if top < modes:
                    y_ref[s, top:, :] = jnp.zeros((modes - top, width), jnp.bfloat16)
                    x_ref[s, :, top:] = jnp.zeros((width, modes - top), jnp.bfloat16)


def smooth(counts, matrices, basis):
    total, width, modes = basis.shape
    slots = 2 - total % 2
    at = lambda i, c: (i, 0, 0)
    return pl.pallas_call(
        smooth_kernel,
        grid_spec=pltpu.PrefetchScalarGridSpec(
            num_scalar_prefetch=1,
            grid=(total // slots,),
            in_specs=[
                pl.BlockSpec((slots, width, width), at),
                pl.BlockSpec((slots, width, modes), at),
            ],
            out_specs=[
                pl.BlockSpec((slots, width, modes), at),
                pl.BlockSpec((slots, modes, width), at),
            ],
        ),
        out_shape=[
            jax.ShapeDtypeStruct((total, width, modes), jnp.bfloat16),
            jax.ShapeDtypeStruct((total, modes, width), jnp.bfloat16),
        ],
        cost_estimate=pl.CostEstimate(
            flops=14 * total * width * width * modes,
            bytes_accessed=2 * total * width * (width + 3 * modes),
            transcendentals=0,
        ),
    )(counts, matrices, basis)


def pick_kernel(wanted, x_ref, *refs):
    refs[-1][...] = x_ref[...]


def pick(wanted, begin, n, x, after):
    _, width, modes = x.shape
    return pl.pallas_call(
        pick_kernel,
        grid_spec=pltpu.PrefetchScalarGridSpec(
            num_scalar_prefetch=1,
            grid=(n,),
            in_specs=[pl.BlockSpec((1, width, modes), lambda i, w: (w[begin + i], 0, 0))]
            + [ANY] * len(after),
            out_specs=pl.BlockSpec((1, width, modes), lambda i, w: (i, 0, 0)),
        ),
        out_shape=jax.ShapeDtypeStruct((n, width, modes), jnp.bfloat16),
        cost_estimate=pl.CostEstimate(
            flops=0, bytes_accessed=4 * n * width * modes, transcendentals=0
        ),
    )(wanted, x, *after)


def block_kernel(begin, n, order, x_ref, y_ref, low_ref, *refs):
    outs, (x_buf, y_buf, low_buf, sems) = refs[:n], refs[n:]
    scale = 1.0 / math.sqrt(x_ref.shape[1])

    def loads(i):
        g = order[begin + i]
        return (
            pltpu.make_async_copy(y_ref.at[g], y_buf.at[i], sems.at[0, i]),
            pltpu.make_async_copy(x_ref.at[g], x_buf.at[i], sems.at[1, i]),
            pltpu.make_async_copy(low_ref.at[i], low_buf.at[i], sems.at[2, i]),
        )

    for i in range(n):
        for copy in loads(i):
            copy.start()
    for i, out in enumerate(outs):
        for copy in loads(i):
            copy.wait()
        y = y_buf[i]
        pair = jnp.dot(y, low_buf[i], preferred_element_type=jnp.float32).astype(jnp.bfloat16)
        own = jnp.dot(y, x_buf[i], preferred_element_type=jnp.float32)
        out[0] = ((own + pair.astype(jnp.float32)) * scale).astype(jnp.bfloat16)


def blocks(order, begin, n, x, y, low):
    _, width, modes = x.shape
    return pl.pallas_call(
        functools.partial(block_kernel, begin, n),
        in_specs=[SMEM, HBM, HBM, ANY],
        out_specs=[VMEM] * n,
        out_shape=[jax.ShapeDtypeStruct((1, modes, modes), jnp.bfloat16)] * n,
        scratch_shapes=[
            pltpu.VMEM((n, width, modes), jnp.bfloat16),
            pltpu.VMEM((n, modes, width), jnp.bfloat16),
            pltpu.VMEM((n, width, modes), jnp.bfloat16),
            pltpu.SemaphoreType.DMA((3, n)),
        ],
        cost_estimate=pl.CostEstimate(
            flops=4 * n * width * modes * modes,
            bytes_accessed=2 * n * modes * (3 * width + modes),
            transcendentals=0,
        ),
    )(order, x, y, low)


def place_kernel(n, where, *refs):
    pieces, out, sems = refs[:n], refs[-2], refs[-1]
    copies = [
        pltpu.make_async_copy(piece.at[0], out.at[where[i]], sems.at[i])
        for i, piece in enumerate(pieces)
    ]
    for copy in copies:
        copy.start()
    for copy in copies:
        copy.wait()


def place(where, pieces, total, before):
    n = len(pieces)
    modes = pieces[0].shape[1]
    chained = [] if before is None else [before]
    return pl.pallas_call(
        functools.partial(place_kernel, n),
        in_specs=[SMEM] + [VMEM] * n + [ANY] * len(chained),
        out_specs=ANY,
        out_shape=jax.ShapeDtypeStruct((total, modes, modes), jnp.bfloat16),
        scratch_shapes=[pltpu.SemaphoreType.DMA((n,))],
        input_output_aliases={} if before is None else {n + 1: 0},
        cost_estimate=pl.CostEstimate(
            flops=0, bytes_accessed=4 * n * modes * modes, transcendentals=0
        ),
    )(where, *pieces, *chained)


def body(matrices, basis_cols, mode_counts, task_map, neighbour):
    total, width, modes = basis_cols.shape
    columns, rows = lax.axis_size("ay"), lax.axis_size("ax")
    me = lax.axis_index("ay").astype(jnp.int32)
    paired = columns & (columns - 1) == 0
    half = columns // 2
    steps = tuple(range(half, columns)) + tuple(range(half - 1, -1, -1))
    hops = jnp.array(steps, jnp.int32)
    targets = me ^ hops if paired else lax.rem(me + hops, columns)
    sources = me ^ hops if paired else lax.rem(me - hops + columns, columns)

    hit = task_map[:, None] == targets[None, :]
    numbers = lax.broadcasted_iota(jnp.int32, hit.shape, 0)
    order = jnp.sum(jnp.where(hit, numbers, 0), axis=0)
    wanted = jnp.sum(jnp.where(hit, neighbour[:, None], 0), axis=0)
    wanted = lax.ppermute(wanted, "ax", [(i + 1, i) for i in range(rows - 1)])

    x, y = smooth(mode_counts, matrices, basis_cols)
    cuts = (0, columns // 4, columns // 4 + 3 * columns // 8, columns)
    spans = list(zip(cuts[:-1], cuts[1:]))
    up = [(i, i + 1) for i in range(rows - 1)]

    def fetch(j, after):
        a, b = spans[j]
        chosen = pick(wanted, a, b - a, x, after)
        return chosen, in_vmem(lax.ppermute(chosen, "ax", up))

    first, low = fetch(0, [])
    second, low_next = fetch(1, [first])
    lows, coarse = [low, low_next], None
    for j, (a, b) in enumerate(spans):
        made = blocks(order, a, b - a, x, y, lows[j])
        if j == 0:
            lows.append(fetch(2, [second, made[-1]])[1])
        arrived = []
        for k, block in zip(steps[a:b], made):
            if k:
                pairs = [(i, i ^ k if paired else (i + k) % columns) for i in range(columns)]
                block = lax.ppermute(block, "ay", pairs)
            arrived.append(in_vmem(block))
        coarse = place(sources[a:b], arrived, total, coarse)
    return x, coarse


def solution(mesh):
    agg = P(("ax", "ay"), None, None)
    flat = P(("ax", "ay"))
    return jax.shard_map(
        body,
        mesh=mesh,
        in_specs=(agg, agg, flat, flat, flat),
        out_specs=(agg, agg),
        check_vma=False,
    )
```

```python
import functools
import math

import jax
import jax.numpy as jnp
from jax import lax
from jax.experimental import pallas as pl
from jax.experimental.pallas import tpu as pltpu
from jax.sharding import PartitionSpec as P


TILE = 128
omegas = (0.3, 0.25, 0.2, 0.3, 0.25, 0.2)

SMEM = pl.BlockSpec(memory_space=pltpu.SMEM)
VMEM = pl.BlockSpec(memory_space=pltpu.VMEM)
ANY = pl.BlockSpec(memory_space=pl.ANY)


def limit(mib):
    return pltpu.CompilerParams(vmem_limit_bytes=mib << 20)


def in_hbm(array):
    return pltpu.with_memory_space_constraint(array, pltpu.HBM)


def in_vmem(array):
    return pltpu.with_memory_space_constraint(array, pltpu.VMEM)


class Route:
    def __init__(self, columns):
        half = columns // 2
        self.columns = columns
        self.paired = columns & (columns - 1) == 0
        self.steps = tuple(range(half, columns)) + tuple(range(half - 1, -1, -1))

    def to(self, me, k):
        return me ^ k if self.paired else (me + k) % self.columns

    def back(self, me, k):
        return me ^ k if self.paired else (me - k + self.columns) % self.columns

    def pairs(self, k):
        return [(i, self.to(i, k)) for i in range(self.columns)]

    def slot(self, table, me, j):
        target = self.to(me, self.steps[j])
        found = jnp.int32(0)
        for s in range(self.columns):
            found = jnp.where(table[s] == target, s, found)
        return found


def smooth_kernel(route, cuts, counts, above, me, a_ref, b_ref, x_ref, xv_ref, y_ref, *refs):
    sent, (sems,) = refs[:-1], refs[-1:]
    slots, width, modes = b_ref.shape
    step = pl.program_id(0)
    first = step * slots
    mine = [counts[first + s] for s in range(slots)]
    groups = pl.cdiv(functools.reduce(jnp.maximum, mine), TILE)
    for live in range(1, modes // TILE + 1):

        @pl.when(groups == live)
        def _():
            top = live * TILE
            rows = lax.broadcasted_iota(jnp.int32, (top, width), 0)
            zero = jnp.zeros((), jnp.bfloat16)
            current = [
                jnp.where(rows < mine[s], b_ref[s, :, :top].T, zero) for s in range(slots)
            ]
            for weight in omegas:
                product = [
                    jnp.dot(current[s], a_ref[s], preferred_element_type=jnp.float32)
                    for s in range(slots)
                ]
                current = [
                    (c.astype(jnp.float32) - weight * p).astype(jnp.bfloat16)
                    for c, p in zip(current, product)
                ]
            for s, c in enumerate(current):
                image = jnp.dot(c, a_ref[s], preferred_element_type=jnp.float32)
                y_ref[first + s, :top, :] = image.astype(jnp.bfloat16)
                xv_ref[first + s, :, :top] = c.T
                if top < modes:
                    y_ref[first + s, top:, :] = jnp.zeros((modes - top, width), jnp.bfloat16)
                    xv_ref[first + s, :, top:] = jnp.zeros((width, modes - top), jnp.bfloat16)

    x_ref[...] = xv_ref[pl.ds(first, slots)]

    columns = route.columns
    copies = []
    for out, a, b in zip(sent, cuts[:-1], cuts[1:]):
        for j in range(a, b):
            wanted = above[columns + route.slot(above, me[0], j)]
            copy = pltpu.make_async_copy(xv_ref.at[wanted], out.at[j - a], sems.at[j])
            copies.append(copy)

            @pl.when(wanted // slots == step)
            def _():
                copy.start()

    @pl.when(step == pl.num_programs(0) - 1)
    def _():
        for copy in copies:
            copy.wait()


def smooth(route, cuts, counts, above, me, matrices, basis):
    total, width, modes = basis.shape
    slots = 2 - total % 2
    at = lambda i, *_: (i, 0, 0)
    spans = [b - a for a, b in zip(cuts[:-1], cuts[1:])]
    return pl.pallas_call(
        functools.partial(smooth_kernel, route, cuts),
        grid_spec=pltpu.PrefetchScalarGridSpec(
            num_scalar_prefetch=3,
            grid=(total // slots,),
            in_specs=[
                pl.BlockSpec((slots, width, width), at),
                pl.BlockSpec((slots, width, modes), at),
            ],
            out_specs=[pl.BlockSpec((slots, width, modes), at), VMEM, VMEM] + [ANY] * len(spans),
            scratch_shapes=[pltpu.SemaphoreType.DMA((total,))],
        ),
        out_shape=[
            jax.ShapeDtypeStruct((total, width, modes), jnp.bfloat16),
            pltpu.VMEM((total, width, modes), jnp.bfloat16),
            pltpu.VMEM((total, modes, width), jnp.bfloat16),
        ]
        + [jax.ShapeDtypeStruct((n, width, modes), jnp.bfloat16) for n in spans],
        compiler_params=limit(24),
        cost_estimate=pl.CostEstimate(
            flops=14 * total * width * width * modes,
            bytes_accessed=2 * total * width * (width + 3 * modes),
            transcendentals=0,
        ),
    )(counts, above, me, in_hbm(matrices), in_hbm(basis))


def block_kernel(route, begin, task, me, x_ref, y_ref, low_ref, *outs):
    scale = 1.0 / math.sqrt(x_ref.shape[1])
    for i, out in enumerate(outs):
        g = route.slot(task, me[0], begin + i)
        y = y_ref[g]
        pair = jnp.dot(y, low_ref[i], preferred_element_type=jnp.float32).astype(jnp.bfloat16)
        own = jnp.dot(y, x_ref[g], preferred_element_type=jnp.float32)
        out[0] = ((own + pair.astype(jnp.float32)) * scale).astype(jnp.bfloat16)


def blocks(route, begin, n, task, me, x, y, low):
    _, width, modes = x.shape
    return pl.pallas_call(
        functools.partial(block_kernel, route, begin),
        in_specs=[SMEM, SMEM, VMEM, VMEM, VMEM],
        out_specs=[VMEM] * n,
        out_shape=[jax.ShapeDtypeStruct((1, modes, modes), jnp.bfloat16)] * n,
        compiler_params=limit(16),
        cost_estimate=pl.CostEstimate(
            flops=4 * n * width * modes * modes,
            bytes_accessed=2 * n * modes * (3 * width + modes),
            transcendentals=0,
        ),
    )(task, me, in_vmem(x), in_vmem(y), in_vmem(low))


def place_kernel(route, me, *refs):
    pieces, out, sems = refs[:-2], refs[-2], refs[-1]
    copies = [
        pltpu.make_async_copy(piece.at[0], out.at[route.back(me[0], k)], sems.at[i])
        for i, (k, piece) in enumerate(zip(route.steps, pieces))
    ]
    for copy in copies:
        copy.start()
    for copy in copies:
        copy.wait()


def place(route, me, pieces):
    n = len(pieces)
    modes = pieces[0].shape[1]
    return pl.pallas_call(
        functools.partial(place_kernel, route),
        in_specs=[SMEM] + [VMEM] * n,
        out_specs=ANY,
        out_shape=jax.ShapeDtypeStruct((n, modes, modes), jnp.bfloat16),
        scratch_shapes=[pltpu.SemaphoreType.DMA((n,))],
        compiler_params=limit(8),
        cost_estimate=pl.CostEstimate(
            flops=0, bytes_accessed=4 * n * modes * modes, transcendentals=0
        ),
    )(me, *[in_vmem(piece) for piece in pieces])


def body(matrices, basis_cols, mode_counts, task_map, neighbour):
    columns, rows = lax.axis_size("ay"), lax.axis_size("ax")
    route = Route(columns)
    me = lax.axis_index("ay").astype(jnp.int32).reshape(1)
    down = [(i + 1, i) for i in range(rows - 1)]
    up = [(i, i + 1) for i in range(rows - 1)]
    cuts = (0, columns // 4, columns // 4 + 3 * columns // 8, columns)

    above = lax.ppermute(jnp.concatenate([task_map, neighbour]), "ax", down)
    out, x, y, *sent = smooth(route, cuts, mode_counts, above, me, matrices, basis_cols)
    lows = []
    for chosen in sent:
        lows.append(lax.ppermute(chosen, "ax", up))
    arrived = []
    for a, b, low in zip(cuts[:-1], cuts[1:], lows):
        made = blocks(route, a, b - a, task_map, me, x, y, low)
        for j, block in zip(range(a, b), made):
            if route.steps[j]:
                block = lax.ppermute(block, "ay", route.pairs(route.steps[j]))
            arrived.append(block)
    return out, place(route, me, arrived)


def solution(mesh):
    agg = P(("ax", "ay"), None, None)
    flat = P(("ax", "ay"))
    return jax.shard_map(
        body,
        mesh=mesh,
        in_specs=(agg, agg, flat, flat, flat),
        out_specs=(agg, agg),
        check_vma=False,
    )
```

```python
import functools
import math

import jax
import jax.numpy as jnp
from jax import lax
from jax.experimental import pallas as pl
from jax.experimental.pallas import tpu as pltpu
from jax.sharding import PartitionSpec as P


TILE = 128
omegas = (0.3, 0.25, 0.2, 0.3, 0.25, 0.2)

SMEM = pl.BlockSpec(memory_space=pltpu.SMEM)
VMEM = pl.BlockSpec(memory_space=pltpu.VMEM)
ANY = pl.BlockSpec(memory_space=pl.ANY)


def limit(mib):
    return pltpu.CompilerParams(vmem_limit_bytes=mib << 20)


def in_hbm(array):
    return pltpu.with_memory_space_constraint(array, pltpu.HBM)


def in_vmem(array):
    return pltpu.with_memory_space_constraint(array, pltpu.VMEM)


class Route:
    def __init__(self, columns):
        half = columns // 2
        self.columns = columns
        self.paired = columns & (columns - 1) == 0
        self.steps = tuple(range(half, columns)) + tuple(range(half - 1, -1, -1))

    def to(self, me, k):
        return me ^ k if self.paired else (me + k) % self.columns

    def back(self, me, k):
        return me ^ k if self.paired else (me - k + self.columns) % self.columns

    def pairs(self, k):
        return [(i, self.to(i, k)) for i in range(self.columns)]

    def slot(self, table, me, j):
        target = self.to(me, self.steps[j])
        found = jnp.int32(0)
        for s in range(self.columns):
            found = jnp.where(table[s] == target, s, found)
        return found


def arrange(route, early, above, task, me, order):
    columns = route.columns
    needed = [route.slot(task, me[0], j) for j in range(early)]
    needed += [above[columns + route.slot(above, me[0], j)] for j in range(early)]
    first = [
        functools.reduce(jnp.maximum, [(n == s).astype(jnp.int32) for n in needed])
        for s in range(columns)
    ]
    ahead, behind = jnp.int32(0), functools.reduce(jnp.add, first)
    for s in range(columns):
        order[jnp.where(first[s] > 0, ahead, behind)] = s
        ahead, behind = ahead + first[s], behind + 1 - first[s]


def smooth_kernel(route, early, begin, n, cuts, above, task, me, counts, a_hbm, b_hbm, *refs):
    chunks = len(cuts) - 1
    refs = refs[3:] if begin else refs
    x_ref, xv_ref, y_ref = refs[:3]
    sent = refs[3 : 3 + chunks]
    order, a_buf, b_buf, in_sems, out_sems, sent_sems = refs[3 + chunks :]
    width, modes = b_buf.shape[1:]
    columns = route.columns
    arrange(route, early, above, task, me, order)

    def loads(p):
        g = order[begin + p]
        return (
            pltpu.make_async_copy(a_hbm.at[g], a_buf.at[p], in_sems.at[0, p]),
            pltpu.make_async_copy(b_hbm.at[g], b_buf.at[p], in_sems.at[1, p]),
        )

    for p in range(n):
        for copy in loads(p):
            copy.start()

    wanted, emits = [], []
    for out, a, b in zip(sent, cuts[:-1], cuts[1:]):
        for j in range(a, b):
            w = above[columns + route.slot(above, me[0], j)]
            wanted.append(w)
            emits.append(
                pltpu.make_async_copy(xv_ref.at[w], out.at[j - a], sent_sems.at[j - cuts[0]])
            )
    for w, emit in zip(wanted, emits):
        if begin:
            known = functools.reduce(jnp.logical_or, [order[p] == w for p in range(begin)])

            @pl.when(known)
            def _():
                emit.start()

    def stored(p):
        g = order[begin + p]
        return pltpu.make_async_copy(xv_ref.at[g], x_ref.at[g], out_sems.at[p])

    @pl.loop(0, n // 2)
    def _(i):
        at = [2 * i, 2 * i + 1]
        slots = [order[begin + p] for p in at]
        for p in at:
            for copy in loads(p):
                copy.wait()
        mine = [counts[g] for g in slots]
        groups = pl.cdiv(jnp.maximum(*mine), TILE)
        for live in range(1, modes // TILE + 1):

            @pl.when(groups == live)
            def _():
                top = live * TILE
                rows = lax.broadcasted_iota(jnp.int32, (top, width), 0)
                zero = jnp.zeros((), jnp.bfloat16)
                current = [
                    jnp.where(rows < count, b_buf[p, :, :top].T, zero)
                    for p, count in zip(at, mine)
                ]
                for weight in omegas:
                    product = [
                        jnp.dot(c, a_buf[p], preferred_element_type=jnp.float32)
                        for p, c in zip(at, current)
                    ]
                    current = [
                        (c.astype(jnp.float32) - weight * d).astype(jnp.bfloat16)
                        for c, d in zip(current, product)
                    ]
                for p, g, c in zip(at, slots, current):
                    image = jnp.dot(c, a_buf[p], preferred_element_type=jnp.float32)
                    y_ref[g, :top, :] = image.astype(jnp.bfloat16)
                    xv_ref[g, :, :top] = c.T
                    if top < modes:
                        y_ref[g, top:, :] = jnp.zeros((modes - top, width), jnp.bfloat16)
                        xv_ref[g, :, top:] = jnp.zeros((width, modes - top), jnp.bfloat16)

        for p in at:
            stored(p).start()
        for w, emit in zip(wanted, emits):

            @pl.when(jnp.logical_or(w == slots[0], w == slots[1]))
            def _():
                emit.start()

    for p in range(n):
        stored(p).wait()
    for emit in emits:
        emit.wait()


def smooth(route, early, begin, n, cuts, above, task, me, counts, matrices, basis, before):
    total, width, modes = basis.shape
    spans = [b - a for a, b in zip(cuts[:-1], cuts[1:])]
    if before:
        before = [before[0], in_vmem(before[1]), in_vmem(before[2])]
    return pl.pallas_call(
        functools.partial(smooth_kernel, route, early, begin, n, cuts),
        in_specs=[SMEM] * 4 + [ANY] * 2 + ([ANY, VMEM, VMEM] if before else []),
        out_specs=[ANY, VMEM, VMEM] + [ANY] * len(spans),
        scratch_shapes=[
            pltpu.SMEM((total,), jnp.int32),
            pltpu.VMEM((n, width, width), jnp.bfloat16),
            pltpu.VMEM((n, width, modes), jnp.bfloat16),
            pltpu.SemaphoreType.DMA((2, n)),
            pltpu.SemaphoreType.DMA((n,)),
            pltpu.SemaphoreType.DMA((cuts[-1] - cuts[0],)),
        ],
        out_shape=[
            jax.ShapeDtypeStruct((total, width, modes), jnp.bfloat16),
            pltpu.VMEM((total, width, modes), jnp.bfloat16),
            pltpu.VMEM((total, modes, width), jnp.bfloat16),
        ]
        + [jax.ShapeDtypeStruct((m, width, modes), jnp.bfloat16) for m in spans],
        input_output_aliases={6: 0, 7: 1, 8: 2} if before else {},
        compiler_params=limit(24),
        cost_estimate=pl.CostEstimate(
            flops=14 * n * width * width * modes,
            bytes_accessed=2 * n * width * (width + 3 * modes),
            transcendentals=0,
        ),
    )(above, task, me, counts, in_hbm(matrices), in_hbm(basis), *before)


def block_kernel(route, begin, task, me, x_ref, y_ref, low_ref, *outs):
    scale = 1.0 / math.sqrt(x_ref.shape[1])
    for i, out in enumerate(outs):
        g = route.slot(task, me[0], begin + i)
        y = y_ref[g]
        pair = jnp.dot(y, low_ref[i], preferred_element_type=jnp.float32).astype(jnp.bfloat16)
        own = jnp.dot(y, x_ref[g], preferred_element_type=jnp.float32)
        out[0] = ((own + pair.astype(jnp.float32)) * scale).astype(jnp.bfloat16)


def blocks(route, begin, n, task, me, x, y, low):
    _, width, modes = x.shape
    return pl.pallas_call(
        functools.partial(block_kernel, route, begin),
        in_specs=[SMEM, SMEM, VMEM, VMEM, VMEM],
        out_specs=[VMEM] * n,
        out_shape=[jax.ShapeDtypeStruct((1, modes, modes), jnp.bfloat16)] * n,
        compiler_params=limit(16),
        cost_estimate=pl.CostEstimate(
            flops=4 * n * width * modes * modes,
            bytes_accessed=2 * n * modes * (3 * width + modes),
            transcendentals=0,
        ),
    )(task, me, in_vmem(x), in_vmem(y), in_vmem(low))


def place_kernel(route, me, *refs):
    pieces, out, sems = refs[:-2], refs[-2], refs[-1]
    copies = [
        pltpu.make_async_copy(piece.at[0], out.at[route.back(me[0], k)], sems.at[i])
        for i, (k, piece) in enumerate(zip(route.steps, pieces))
    ]
    for copy in copies:
        copy.start()
    for copy in copies:
        copy.wait()


def place(route, me, pieces):
    n = len(pieces)
    modes = pieces[0].shape[1]
    return pl.pallas_call(
        functools.partial(place_kernel, route),
        in_specs=[SMEM] + [VMEM] * n,
        out_specs=ANY,
        out_shape=jax.ShapeDtypeStruct((n, modes, modes), jnp.bfloat16),
        scratch_shapes=[pltpu.SemaphoreType.DMA((n,))],
        compiler_params=limit(8),
        cost_estimate=pl.CostEstimate(
            flops=0, bytes_accessed=4 * n * modes * modes, transcendentals=0
        ),
    )(me, *[in_vmem(piece) for piece in pieces])


def body(matrices, basis_cols, mode_counts, task_map, neighbour):
    columns, rows = lax.axis_size("ay"), lax.axis_size("ax")
    route = Route(columns)
    me = lax.axis_index("ay").astype(jnp.int32).reshape(1)
    down = [(i + 1, i) for i in range(rows - 1)]
    up = [(i, i + 1) for i in range(rows - 1)]
    early = columns // 4
    cuts = (0, early, 2 * early, columns)
    half = columns // 2

    above = lax.ppermute(jnp.concatenate([task_map, neighbour]), "ax", down)
    scalars = (above, task_map, me, mode_counts, matrices, basis_cols)
    *kept, first = smooth(route, early, 0, half, cuts[:2], *scalars, [])
    out, x, y, *others = smooth(route, early, half, half, cuts[1:], *scalars, kept)
    lows = []
    for chosen in [first, *others]:
        lows.append(lax.ppermute(chosen, "ax", up))
    arrived = []
    for a, b, low in zip(cuts[:-1], cuts[1:], lows):
        made = blocks(route, a, b - a, task_map, me, x, y, low)
        for j, block in zip(range(a, b), made):
            if route.steps[j]:
                block = lax.ppermute(block, "ay", route.pairs(route.steps[j]))
            arrived.append(block)
    return out, place(route, me, arrived)


def solution(mesh):
    agg = P(("ax", "ay"), None, None)
    flat = P(("ax", "ay"))
    return jax.shard_map(
        body,
        mesh=mesh,
        in_specs=(agg, agg, flat, flat, flat),
        out_specs=(agg, agg),
        check_vma=False,
    )
```

```python
import functools
import math

import jax
import jax.numpy as jnp
from jax import lax
from jax.experimental import pallas as pl
from jax.experimental.pallas import tpu as pltpu
from jax.sharding import PartitionSpec as P


TILE = 128
omegas = (0.3, 0.25, 0.2, 0.3, 0.25, 0.2)

SMEM = pl.BlockSpec(memory_space=pltpu.SMEM)
VMEM = pl.BlockSpec(memory_space=pltpu.VMEM)
ANY = pl.BlockSpec(memory_space=pl.ANY)


def limit(mib):
    return pltpu.CompilerParams(vmem_limit_bytes=mib << 20)


def in_hbm(array):
    return pltpu.with_memory_space_constraint(array, pltpu.HBM)


def in_vmem(array):
    return pltpu.with_memory_space_constraint(array, pltpu.VMEM)


class Route:
    def __init__(self, columns):
        half = columns // 2
        self.columns = columns
        self.paired = columns & (columns - 1) == 0
        self.steps = tuple(range(half, columns)) + tuple(range(half - 1, -1, -1))

    def to(self, me, k):
        return me ^ k if self.paired else (me + k) % self.columns

    def back(self, me, k):
        return me ^ k if self.paired else (me - k + self.columns) % self.columns

    def pairs(self, k):
        return [(i, self.to(i, k)) for i in range(self.columns)]

    def slot(self, table, me, j):
        target = self.to(me, self.steps[j])
        found = jnp.int32(0)
        for s in range(self.columns):
            found = jnp.where(table[s] == target, s, found)
        return found


def load_kernel(a_hbm, b_hbm, a_ref, b_ref, sems):
    copies = []
    for g in range(a_hbm.shape[0]):
        copies.append(pltpu.make_async_copy(a_hbm.at[g], a_ref.at[g], sems.at[0, g]))
        copies.append(pltpu.make_async_copy(b_hbm.at[g], b_ref.at[g], sems.at[1, g]))
    for copy in copies:
        copy.start()
    for copy in copies:
        copy.wait()


def load(matrices, basis):
    return pl.pallas_call(
        load_kernel,
        in_specs=[ANY] * 2,
        out_specs=[VMEM] * 2,
        out_shape=[pltpu.VMEM(a.shape, a.dtype) for a in (matrices, basis)],
        scratch_shapes=[pltpu.SemaphoreType.DMA((2, matrices.shape[0]))],
        compiler_params=limit(8),
        cost_estimate=pl.CostEstimate(
            flops=0, bytes_accessed=2 * (matrices.size + basis.size), transcendentals=0
        ),
    )(in_hbm(matrices), in_hbm(basis))


def arrange(route, local, above, me, order, seen):
    columns = route.columns
    for s in range(columns):
        seen[s] = 0
    listed = []
    for j in range(2):
        listed.append(route.slot(local, me[0], j))
        listed.append(above[columns + route.slot(above, me[0], j)])
    count = jnp.int32(0)
    for s in listed + list(range(columns)):
        fresh = 1 - seen[s]

        @pl.when(fresh == 1)
        def _():
            order[count] = s

        seen[s] = 1
        count = count + fresh


def smooth_kernel(route, begin, n, cuts, waits, local, above, me, a_ref, b_ref, *refs):
    chunks = len(cuts) - 1
    refs = refs[3 + waits :] if begin else refs
    x_ref, xv_ref, y_ref = refs[:3]
    sent = refs[3 : 3 + chunks]
    order, seen, out_sems, sent_sems = refs[3 + chunks :]
    width, modes = b_ref.shape[1:]
    columns = route.columns
    arrange(route, local, above, me, order, seen)

    wanted, emits = [], []
    for out, a, b in zip(sent, cuts[:-1], cuts[1:]):
        for j in range(a, b):
            w = above[columns + route.slot(above, me[0], j)]
            wanted.append(w)
            emits.append(
                pltpu.make_async_copy(xv_ref.at[w], out.at[j - a], sent_sems.at[j - cuts[0]])
            )
    for w, emit in zip(wanted, emits):
        if begin:
            known = functools.reduce(jnp.logical_or, [order[p] == w for p in range(begin)])

            @pl.when(known)
            def _():
                emit.start()

    def stored(p):
        g = order[begin + p]
        return pltpu.make_async_copy(xv_ref.at[g], x_ref.at[g], out_sems.at[p])

    @pl.loop(0, n // 2)
    def _(i):
        at = [2 * i, 2 * i + 1]
        slots = [order[begin + p] for p in at]
        mine = [local[2 * columns + g] for g in slots]
        groups = pl.cdiv(jnp.maximum(*mine), TILE)
        for live in range(1, modes // TILE + 1):

            @pl.when(groups == live)
            def _():
                top = live * TILE
                rows = lax.broadcasted_iota(jnp.int32, (top, width), 0)
                zero = jnp.zeros((), jnp.bfloat16)
                current = [
                    jnp.where(rows < count, b_ref[g, :, :top].T, zero)
                    for g, count in zip(slots, mine)
                ]
                for weight in omegas:
                    product = [
                        jnp.dot(c, a_ref[g], preferred_element_type=jnp.float32)
                        for g, c in zip(slots, current)
                    ]
                    current = [
                        (c.astype(jnp.float32) - weight * d).astype(jnp.bfloat16)
                        for c, d in zip(current, product)
                    ]
                for g, c in zip(slots, current):
                    image = jnp.dot(c, a_ref[g], preferred_element_type=jnp.float32)
                    y_ref[g, :top, :] = image.astype(jnp.bfloat16)
                    xv_ref[g, :, :top] = c.T
                    if top < modes:
                        y_ref[g, top:, :] = jnp.zeros((modes - top, width), jnp.bfloat16)
                        xv_ref[g, :, top:] = jnp.zeros((width, modes - top), jnp.bfloat16)

        for p in at:
            stored(p).start()
        for w, emit in zip(wanted, emits):

            @pl.when(jnp.logical_or(w == slots[0], w == slots[1]))
            def _():
                emit.start()

    for p in range(n):
        stored(p).wait()
    for emit in emits:
        emit.wait()


def smooth(route, begin, n, cuts, local, above, me, matrices, basis, before, after=()):
    total, width, modes = basis.shape
    spans = [b - a for a, b in zip(cuts[:-1], cuts[1:])]
    if before:
        before = [before[0], in_vmem(before[1]), in_vmem(before[2])]
    return pl.pallas_call(
        functools.partial(smooth_kernel, route, begin, n, cuts, len(after)),
        in_specs=[SMEM] * 3
        + [VMEM] * 2
        + ([ANY, VMEM, VMEM] if before else [])
        + [ANY] * len(after),
        out_specs=[ANY, VMEM, VMEM] + [ANY] * len(spans),
        scratch_shapes=[
            pltpu.SMEM((total,), jnp.int32),
            pltpu.SMEM((total,), jnp.int32),
            pltpu.SemaphoreType.DMA((n,)),
            pltpu.SemaphoreType.DMA((cuts[-1] - cuts[0],)),
        ],
        out_shape=[
            jax.ShapeDtypeStruct((total, width, modes), jnp.bfloat16),
            pltpu.VMEM((total, width, modes), jnp.bfloat16),
            pltpu.VMEM((total, modes, width), jnp.bfloat16),
        ]
        + [jax.ShapeDtypeStruct((m, width, modes), jnp.bfloat16) for m in spans],
        input_output_aliases={5: 0, 6: 1, 7: 2} if before else {},
        compiler_params=limit(16),
        cost_estimate=pl.CostEstimate(
            flops=14 * n * width * width * modes,
            bytes_accessed=2 * n * width * (width + 3 * modes),
            transcendentals=0,
        ),
    )(local, above, me, in_vmem(matrices), in_vmem(basis), *before, *after)


def block_kernel(route, begin, task, me, x_ref, y_ref, low_ref, *outs):
    scale = 1.0 / math.sqrt(x_ref.shape[1])
    for i, out in enumerate(outs):
        g = route.slot(task, me[0], begin + i)
        y = y_ref[g]
        pair = jnp.dot(y, low_ref[i], preferred_element_type=jnp.float32).astype(jnp.bfloat16)
        own = jnp.dot(y, x_ref[g], preferred_element_type=jnp.float32)
        out[0] = ((own + pair.astype(jnp.float32)) * scale).astype(jnp.bfloat16)


def blocks(route, begin, n, task, me, x, y, low):
    _, width, modes = x.shape
    return pl.pallas_call(
        functools.partial(block_kernel, route, begin),
        in_specs=[SMEM, SMEM, VMEM, VMEM, VMEM],
        out_specs=[VMEM] * n,
        out_shape=[jax.ShapeDtypeStruct((1, modes, modes), jnp.bfloat16)] * n,
        compiler_params=limit(16),
        cost_estimate=pl.CostEstimate(
            flops=4 * n * width * modes * modes,
            bytes_accessed=2 * n * modes * (3 * width + modes),
            transcendentals=0,
        ),
    )(task, me, in_vmem(x), in_vmem(y), in_vmem(low))


def place_kernel(route, me, *refs):
    pieces, out, sems = refs[:-2], refs[-2], refs[-1]
    copies = [
        pltpu.make_async_copy(piece.at[0], out.at[route.back(me[0], k)], sems.at[i])
        for i, (k, piece) in enumerate(zip(route.steps, pieces))
    ]
    for copy in copies:
        copy.start()
    for copy in copies:
        copy.wait()


def place(route, me, pieces):
    n = len(pieces)
    modes = pieces[0].shape[1]
    return pl.pallas_call(
        functools.partial(place_kernel, route),
        in_specs=[SMEM] + [VMEM] * n,
        out_specs=ANY,
        out_shape=jax.ShapeDtypeStruct((n, modes, modes), jnp.bfloat16),
        scratch_shapes=[pltpu.SemaphoreType.DMA((n,))],
        compiler_params=limit(8),
        cost_estimate=pl.CostEstimate(
            flops=0, bytes_accessed=4 * n * modes * modes, transcendentals=0
        ),
    )(me, *[in_vmem(piece) for piece in pieces])


def body(matrices, basis_cols, mode_counts, task_map, neighbour):
    columns, rows = lax.axis_size("ay"), lax.axis_size("ax")
    route = Route(columns)
    me = lax.axis_index("ay").astype(jnp.int32).reshape(1)
    down = [(i + 1, i) for i in range(rows - 1)]
    up = [(i, i + 1) for i in range(rows - 1)]
    cuts = (0, 1, 2, columns // 2, columns)
    spans = list(zip(cuts[:-1], cuts[1:]))

    local = jnp.concatenate([task_map, neighbour, mode_counts])
    above = lax.ppermute(local, "ax", down)
    loaded = load(matrices, basis_cols)
    scalars = (local, above, me, *loaded)

    def fetch(chosen):
        return lax.ppermute(chosen, "ax", up)

    def exchange(j, x, y, low):
        a, b = spans[j]
        made = blocks(route, a, b - a, local, me, x, y, low)
        pieces = []
        for i, block in zip(range(a, b), made):
            if route.steps[i]:
                block = lax.ppermute(block, "ay", route.pairs(route.steps[i]))
            pieces.append(block)
        return made, pieces

    *kept, chosen = smooth(route, 0, 2, cuts[:2], *scalars, [])
    low0 = fetch(chosen)
    *kept, chosen = smooth(route, 2, 2, cuts[1:3], *scalars, kept)
    low1 = fetch(chosen)
    made0, pieces0 = exchange(0, kept[1], kept[2], low0)
    made1, pieces1 = exchange(1, kept[1], kept[2], low1)
    out, x, y, chosen2, chosen3 = smooth(
        route, 4, columns - 4, cuts[2:], *scalars, kept, [made0[0], made1[0]]
    )
    low2, low3 = fetch(chosen2), fetch(chosen3)
    pieces = pieces0 + pieces1 + exchange(2, x, y, low2)[1] + exchange(3, x, y, low3)[1]
    return out, place(route, me, pieces)


def solution(mesh):
    agg = P(("ax", "ay"), None, None)
    flat = P(("ax", "ay"))
    return jax.shard_map(
        body,
        mesh=mesh,
        in_specs=(agg, agg, flat, flat, flat),
        out_specs=(agg, agg),
        check_vma=False,
    )
```
